512 devices in a mesh: dp: 4 (over x), expert: 128 (over z, y, core).
Axes of the slice: x: 4, y: 8, z: 8, core: 2. Of those that a mesh axis runs over, the one named last changes fastest.
Arguments:
- tokens: bfloat16 [2048, 2048], P('expert', 'dp'), may hold values from -6 to 6
- cotangent: bfloat16 [2048, 2048], P('expert', 'dp'), may hold values from -6 to 6
- expert_ids: int32 [2048, 8], P('expert'), may hold values from 0 to 127, all different within a row; in each aligned block of 16 rows (0 to 15, 16 to 31, ...) at most 2 rows name the same one
- gate_probs: float32 [2048, 8], P('expert'), may hold values from 0.05 to 1
- w_gate: bfloat16 [128, 768, 2048], P('expert', None, 'dp'), may hold values from -0.125 to 0.125
- w_up: bfloat16 [128, 768, 2048], P('expert', None, 'dp'), may hold values from -0.125 to 0.125
- w_down: bfloat16 [128, 768, 2048], P('expert', None, 'dp'), may hold values from -0.21875 to 0.21875
Outputs:
- mixed: bfloat16 [2048, 2048], P('expert', 'dp')
- grad_tokens: bfloat16 [2048, 2048], P('expert', 'dp')
- grad_gate: bfloat16 [128, 768, 2048], P('expert', None, 'dp')
- grad_up: bfloat16 [128, 768, 2048], P('expert', None, 'dp')
- grad_down: bfloat16 [128, 768, 2048], P('expert', None, 'dp')
The draws below stay inside these ranges and needn't reach their ends.
Inputs may be any that keep to these rules, and one draw needn't show every extreme that they name: `expert_ids`: each token names 8 different experts. The 16 tokens of one index of expert (rows b * 16 to (b + 1) * 16 - 1) name no expert more than 2 times, a bound that some block reaches.
All inputs are finite; a program needn't handle non-finite values.
Results may differ from the reference program's by a relative error of at most 0.02.
Values may be sent and summed in bfloat16 or wider, within the bound.
A program may use at most 64 MiB of HBM per device.

```python
import math
import jax
import jax.numpy as jnp
import numpy as np
from jax import lax

D = 2048
FF = 768
TOPK = 8
TOK_DEV = 16
EXPERTS = 128
CAP = 2
TOKENS = 2048
N_DP = 4


def block_scale(own_key, extent, shards, low, top_value):
    def one(axis_at, blocks):
        draws = jax.random.uniform(jax.random.fold_in(jax.random.fold_in(own_key, 6), axis_at), (blocks,), jnp.float32, low / len(shards), top_value / len(shards))
        return jnp.repeat(jnp.exp(draws), extent[axis_at] // blocks).reshape((-1,) + (1,) * (len(extent) - axis_at - 1))

    level = one(*shards[0])
    for cut in shards[1:]:
        level = level * one(*cut)
    return level


def routed_block(rng, own, number, rows, number_of, top, most, slope):
    order = jax.random.permutation(rng, number_of)
    crowded, common = shares(number_of, rows * top, most, slope, True), shares(number_of, rows * top, most, slope, False)
    places = jnp.arange(number_of)

    def named(lengths, rotation):
        used = int((lengths > 0).sum())
        fixed = max(1, used // 4)
        passed = fixed + (places - fixed + rotation * (used - fixed)) % max(1, number_of - fixed)
        return jnp.zeros((number_of,), jnp.int32).at[order[jnp.where(places < fixed, places, passed)]].set(jnp.asarray(lengths, jnp.int32))

    lengths = jnp.where(number % 4 == 0, named(crowded, number // 4), named(common, number - number // 4 - 1))
    mixed = jax.random.permutation(jax.random.fold_in(own, 3), number_of)
    giver, receiver = mixed[0:number_of // 2 * 2:2], mixed[1:number_of // 2 * 2:2]
    margin = jnp.minimum(lengths[giver] - 1, most - lengths[receiver]) // 2
    margin = jnp.where((giver == order[0]) | (receiver == order[0]) | (lengths[receiver] == 0), 0, jnp.maximum(margin, 0))
    passed = jax.random.randint(jax.random.fold_in(own, 4), (number_of // 2,), 0, 1 << 20) % (margin + 1)
    lengths = lengths.at[giver].add(-passed).at[receiver].add(passed)
    members = jnp.searchsorted(jnp.cumsum(lengths), jnp.arange(rows * top), side="right").astype(jnp.int32)
    listing = members.reshape(top, rows).T
    listing = listing[jax.random.permutation(jax.random.fold_in(own, 1), rows)]
    rotation = jax.random.randint(jax.random.fold_in(own, 2), (rows, 1), 0, top)
    return jnp.take_along_axis(listing, (jnp.arange(top)[None, :] + rotation) % top, axis=1)


def shares(count, total, most, lean, full):
    portions = [(1 << 20) // math.isqrt(rank ** lean) + 1 for rank in range(1, count + 1)]
    largest = most if full else min(most, max(-(-total // count), total * portions[0] // sum(portions)))
    least = 1 if total - largest >= count - 1 else 0
    counts, rest = [largest] + [least] * (count - 1), total - largest - least * (count - 1)
    while rest > 0:
        movable = [i for i in range(1, count) if counts[i] < largest] or [i for i in range(1, count) if counts[i] < most]
        mass, left = sum([portions[i] for i in movable]), rest
        for i in movable:
            addition = min(most - counts[i], max(1, left * portions[i] // mass), rest)
            counts[i] = counts[i] + addition
            rest = rest - addition
    return np.array(counts)


def centred(key, dims, scale, most, pieces=(), kind=jnp.bfloat16):
    values = scale * jax.random.normal(key, dims, jnp.float32)
    if pieces:
        values = values * block_scale(key, dims, pieces, -0.22, 0.18)
    return jnp.clip(values, -most, most).astype(kind)


def setup_inputs(seed: int = 0) -> dict:
    splits = jax.random.split(jax.random.key(seed), 8)
    tokens = centred(splits[0], (TOKENS, D), 1.0, 6.0, ((0, 128), (1, 4)))
    cotangent = centred(splits[1], (TOKENS, D), 1.0, 6.0, ((0, 128), (1, 4)))
    expert_ids_keys = jax.random.split(jax.random.fold_in(splits[2], 1), TOKENS // TOK_DEV)
    expert_ids_turns = jax.random.permutation(jax.random.fold_in(splits[2], 3), TOKENS // TOK_DEV)
    expert_ids = jax.vmap(lambda own, number: routed_block(jax.random.fold_in(splits[2], 2), own, number, TOK_DEV, EXPERTS, TOPK, CAP, 2))(expert_ids_keys, expert_ids_turns).reshape((TOKENS, TOPK))
    gate_probs = jnp.clip(jnp.exp(math.log(1.0) - 2.9957323 * jax.random.uniform(splits[3], (TOKENS, TOPK), jnp.float32) ** block_scale(splits[3], (TOKENS, TOPK), ((0, 128),), -0.2, 0.2)), 0.05, 1.0)
    w_gate = centred(splits[4], (EXPERTS, FF, D), D ** -0.5, 0.125, ((0, 128), (2, 4)))
    w_up = centred(splits[5], (EXPERTS, FF, D), D ** -0.5, 0.125, ((0, 128), (2, 4)))
    w_down = centred(splits[6], (EXPERTS, FF, D), FF ** -0.5, 0.21875, ((0, 128), (2, 4)))
    return {"tokens": tokens, "cotangent": cotangent, "expert_ids": expert_ids, "gate_probs": gate_probs, "w_gate": w_gate, "w_up": w_up, "w_down": w_down}


def activate(pre_gate, pre_up, back_hidden):
    sigmas = jax.nn.sigmoid(pre_gate)
    silu_vals = pre_gate * sigmas
    hidden = (silu_vals * pre_up).astype(jnp.bfloat16)
    back_gate = (back_hidden * pre_up * sigmas * (1.0 + pre_gate * (1.0 - sigmas))).astype(jnp.bfloat16)
    back_up = (back_hidden * silu_vals).astype(jnp.bfloat16)
    return hidden, back_gate, back_up


def block_sums(rows, matrix):
    count = rows.shape[0]
    width = D // N_DP
    left = rows.astype(jnp.float32).reshape(count, N_DP, width)
    right = matrix.astype(jnp.float32).reshape(matrix.shape[0], N_DP, width)
    parts = jnp.einsum("snd,fnd->nsf", left, right, precision=lax.Precision.HIGHEST)
    parts = parts.astype(jnp.bfloat16).astype(jnp.float32)
    return jnp.sum(parts, axis=0)


def reference(tokens, cotangent, expert_ids, gate_probs, w_gate, w_up, w_down):
    blocks = TOKENS // TOK_DEV
    chosen = expert_ids.reshape(blocks, TOK_DEV * TOPK).astype(jnp.int32)
    onehot = (chosen[:, :, None] == jnp.arange(EXPERTS, dtype=jnp.int32)[None, None, :]).astype(jnp.int32)
    before = jnp.cumsum(onehot, axis=1) - onehot
    ranks = jnp.sum(before * onehot, axis=2).astype(jnp.int32)
    block_ids = jnp.broadcast_to(jnp.arange(blocks, dtype=jnp.int32)[:, None], chosen.shape)
    token_ids = block_ids * TOK_DEV + (jnp.arange(TOK_DEV * TOPK, dtype=jnp.int32) // TOPK)[None, :]
    slot_table = jnp.full((EXPERTS, blocks, CAP), TOKENS, jnp.int32).at[chosen, block_ids, ranks].set(token_ids)
    prob_table = jnp.zeros((EXPERTS, blocks, CAP), jnp.float32).at[chosen, block_ids, ranks].set(
        gate_probs.reshape(blocks, TOK_DEV * TOPK).astype(jnp.float32))
    padded_x = jnp.concatenate([tokens, jnp.zeros((1, D), tokens.dtype)], axis=0)
    padded_dy = jnp.concatenate([cotangent.astype(jnp.float32), jnp.zeros((1, D), jnp.float32)], axis=0)
    contract_rows = (((0,), (0,)), ((), ()))

    def one_expert(packed):
        row_ids, row_probs, gate_mat, up_mat, down_mat = packed
        row_ids = row_ids.reshape(-1)
        row_probs = row_probs.reshape(-1)
        x_rows = padded_x[row_ids]
        back_row = (row_probs[:, None] * padded_dy[row_ids]).astype(jnp.bfloat16)
        pre_gate = block_sums(x_rows, gate_mat)
        pre_up = block_sums(x_rows, up_mat)
        back_hidden = block_sums(back_row, down_mat)
        hidden, back_gate, back_up = activate(pre_gate, pre_up, back_hidden)
        expert_out = jnp.dot(hidden, down_mat, preferred_element_type=jnp.float32).astype(jnp.bfloat16)
        back_rows = (jnp.dot(back_gate, gate_mat, preferred_element_type=jnp.float32)
                     + jnp.dot(back_up, up_mat, preferred_element_type=jnp.float32)).astype(jnp.bfloat16)
        grad_gate = lax.dot_general(back_gate, x_rows, contract_rows, preferred_element_type=jnp.float32).astype(jnp.bfloat16)
        grad_up = lax.dot_general(back_up, x_rows, contract_rows, preferred_element_type=jnp.float32).astype(jnp.bfloat16)
        grad_down = lax.dot_general(hidden, back_row, contract_rows, preferred_element_type=jnp.float32).astype(jnp.bfloat16)
        return expert_out, back_rows, grad_gate, grad_up, grad_down

    expert_out, back_rows, grad_gate, grad_up, grad_down = lax.map(
        one_expert, (slot_table, prob_table, w_gate, w_up, w_down))
    flat_rows = slot_table.reshape(-1)
    flat_probs = prob_table.reshape(-1)
    mixed = jnp.zeros((TOKENS + 1, D), jnp.float32).at[flat_rows].add(
        flat_probs[:, None] * expert_out.reshape(-1, D).astype(jnp.float32))
    grad_tokens = jnp.zeros((TOKENS + 1, D), jnp.float32).at[flat_rows].add(
        back_rows.reshape(-1, D).astype(jnp.float32))
    return (mixed[:TOKENS].astype(jnp.bfloat16), grad_tokens[:TOKENS].astype(jnp.bfloat16),
            grad_gate, grad_up, grad_down)
```

```python
import jax
import jax.numpy as jnp
from jax import lax
from jax.experimental import pallas as pl
from jax.experimental.pallas import tpu as pltpu
from jax.sharding import PartitionSpec as P


def activate(pre_gate, pre_up, back_hidden):
    sigmas = jax.nn.sigmoid(pre_gate)
    silu_vals = pre_gate * sigmas
    hidden = (silu_vals * pre_up).astype(jnp.bfloat16)
    back_gate = (back_hidden * pre_up * sigmas * (1.0 + pre_gate * (1.0 - sigmas))).astype(
        jnp.bfloat16
    )
    back_up = (back_hidden * silu_vals).astype(jnp.bfloat16)
    return (hidden, back_gate, back_up)


MESH = pl.DeviceIdType.MESH


def wait_bytes(ref, sem):
    pltpu.make_async_copy(ref, ref, sem).wait()


def exchange(src, dst, send_sem, recv_sem, local_sem, ready):
    x, e = lax.axis_index("dp"), lax.axis_index("expert")
    z, y, c = e // 16, (e // 2) % 8, e % 2

    def peer(dz, dy, dc):
        return lax.rem(z + dz, 8) * 16 + lax.rem(y + dy, 8) * 2 + lax.rem(c + dc, 2)

    def greet(sem, dz, dy, dc):
        pl.semaphore_signal(sem, inc=1, device_id=(x, peer(dz, dy, dc)), device_id_type=MESH)

    def send(dz, dy, dc):
        p = peer(dz, dy, dc)
        pltpu.make_async_remote_copy(
            src_ref=src.at[p],
            dst_ref=dst.at[e],
            send_sem=send_sem,
            recv_sem=recv_sem,
            device_id=(x, p),
            device_id_type=MESH,
        ).start()

    barrier = pltpu.get_barrier_semaphore()
    for dz in range(1, 8):
        greet(barrier, dz, 0, 0)
    for i in range(1, 16):
        greet(barrier, 0, i // 2, i % 2)
    keep = pltpu.make_async_copy(src.at[e], dst.at[e], local_sem)
    keep.start()
    pl.semaphore_wait(barrier, 22)
    for dz in range(1, 8):
        greet(ready, dz, 0, 0)
    for i in range(1, 16):
        send(0, i // 2, i % 2)
    for dz in range(1, 8):
        send(dz, 0, 0)
    pl.semaphore_wait(ready, 7)

    def far(i, carry):
        i = lax.rem(i * 11, 105)
        j = i % 15 + 1
        send(i // 15 + 1, j // 2, j % 2)
        return carry

    lax.fori_loop(0, 105, far, 0)
    keep.wait()
    wait_bytes(src.at[pl.ds(0, 127)], send_sem)
    wait_bytes(dst.at[pl.ds(0, 127)], recv_sem)


def deliver(outbound):
    shape = outbound.shape
    flat = outbound.reshape(128, 16, 128)
    out = pl.pallas_call(
        exchange,
        out_shape=jax.ShapeDtypeStruct(flat.shape, flat.dtype),
        in_specs=[pl.BlockSpec(memory_space=pltpu.VMEM)],
        out_specs=pl.BlockSpec(memory_space=pltpu.VMEM),
        scratch_shapes=[
            pltpu.SemaphoreType.DMA,
            pltpu.SemaphoreType.DMA,
            pltpu.SemaphoreType.DMA,
            pltpu.SemaphoreType.REGULAR,
        ],
        compiler_params=pltpu.CompilerParams(collective_id=0, has_side_effects=True),
    )(flat)
    return out.reshape(shape)


def on_device(tokens, cotangent, expert_ids, gate_probs, w_gate, w_up, w_down):
    tok_rows, columns = tokens.shape
    top_count = expert_ids.shape[1]
    experts = lax.axis_size("expert")
    capacity = min(tok_rows, max(2, 2 * tok_rows * top_count // experts))
    slot_count = experts * capacity
    flat_ids = expert_ids.reshape(-1)
    onehot = (flat_ids[:, None] == jnp.arange(experts, dtype=jnp.int32)[None, :]).astype(jnp.int32)
    before = jnp.cumsum(onehot, axis=0) - onehot
    ranks = jnp.sum(before * onehot, axis=1)
    slot_ids = flat_ids * capacity + ranks
    chosen = (slot_ids[:, None] == jnp.arange(slot_count, dtype=jnp.int32)[None, :]).astype(
        jnp.float32
    )
    chosen = chosen.reshape(tok_rows, top_count, slot_count)
    select = jnp.sum(chosen, axis=1)
    weighted = jnp.sum(chosen * gate_probs[:, :, None], axis=1)
    contract_rows = (((0,), (0,)), ((), ()))
    contract_cols = (((1,), (1,)), ((), ()))
    x_rows = lax.dot_general(
        select.astype(jnp.bfloat16), tokens, contract_rows, preferred_element_type=jnp.float32
    ).astype(jnp.bfloat16)
    back_row = lax.dot_general(
        weighted,
        cotangent.astype(jnp.float32),
        contract_rows,
        precision=lax.Precision.HIGHEST,
        preferred_element_type=jnp.float32,
    ).astype(jnp.bfloat16)
    outbound = jnp.stack([x_rows, back_row], axis=1).reshape(experts, capacity, 2, columns)
    inbound = deliver(outbound).reshape(slot_count, 2, columns)
    x_in = inbound[:, 0]
    d_in = inbound[:, 1]
    gate_mat = w_gate[0]
    up_mat = w_up[0]
    down_mat = w_down[0]
    part_gate = lax.dot_general(x_in, gate_mat, contract_cols, preferred_element_type=jnp.float32)
    part_up = lax.dot_general(x_in, up_mat, contract_cols, preferred_element_type=jnp.float32)
    part_back = lax.dot_general(d_in, down_mat, contract_cols, preferred_element_type=jnp.float32)
    pre_gate, pre_up, back_hidden = (
        lax.psum(part_gate.astype(jnp.bfloat16), "dp").astype(jnp.float32),
        lax.psum(part_up.astype(jnp.bfloat16), "dp").astype(jnp.float32),
        lax.psum(part_back.astype(jnp.bfloat16), "dp").astype(jnp.float32),
    )
    hidden, back_gate, back_up = activate(pre_gate, pre_up, back_hidden)
    expert_out = jnp.dot(hidden, down_mat, preferred_element_type=jnp.float32).astype(jnp.bfloat16)
    back_rows = (
        jnp.dot(back_gate, gate_mat, preferred_element_type=jnp.float32)
        + jnp.dot(back_up, up_mat, preferred_element_type=jnp.float32)
    ).astype(jnp.bfloat16)
    grad_gate = lax.dot_general(
        back_gate, x_in, contract_rows, preferred_element_type=jnp.float32
    ).astype(jnp.bfloat16)
    grad_up = lax.dot_general(
        back_up, x_in, contract_rows, preferred_element_type=jnp.float32
    ).astype(jnp.bfloat16)
    grad_down = lax.dot_general(
        hidden, d_in, contract_rows, preferred_element_type=jnp.float32
    ).astype(jnp.bfloat16)
    homeward = jnp.stack([expert_out, back_rows], axis=1).reshape(experts, capacity, 2, columns)
    returned = deliver(homeward).reshape(slot_count, 2, columns)
    mixed = jnp.dot(
        weighted,
        returned[:, 0].astype(jnp.float32),
        precision=lax.Precision.HIGHEST,
        preferred_element_type=jnp.float32,
    ).astype(jnp.bfloat16)
    grad_tokens = jnp.dot(
        select.astype(jnp.bfloat16), returned[:, 1], preferred_element_type=jnp.float32
    ).astype(jnp.bfloat16)
    return (mixed, grad_tokens, grad_gate[None], grad_up[None], grad_down[None])


def solution(mesh):
    in_specs = (
        P("expert", "dp"),
        P("expert", "dp"),
        P("expert", None),
        P("expert", None),
        P("expert", None, "dp"),
        P("expert", None, "dp"),
        P("expert", None, "dp"),
    )
    out_specs = (
        P("expert", "dp"),
        P("expert", "dp"),
        P("expert", None, "dp"),
        P("expert", None, "dp"),
        P("expert", None, "dp"),
    )
    return jax.shard_map(
        on_device, mesh=mesh, in_specs=in_specs, out_specs=out_specs, check_vma=False
    )
```

```python
import functools

import jax
import jax.numpy as jnp
from jax import lax
from jax.experimental import pallas as pl
from jax.experimental.pallas import tpu as pltpu
from jax.sharding import PartitionSpec as P

MESH = pl.DeviceIdType.MESH
BF16 = jnp.bfloat16
F32 = jnp.float32
CHUNKS = 4
SOURCES = 128 // CHUNKS
ROWS = 2 * SOURCES
PIECE = ROWS // 4
ORDER = (0, 1, 7, 2, 6, 3, 5, 4)
COLUMNS = 512
FF = 768
WIDE = 3 * FF
HALF = WIDE // 2


def wait_bytes(ref, sem):
    pltpu.make_async_copy(ref, ref, sem).wait()


def dot(a, b):
    return jnp.dot(a, b, preferred_element_type=F32)


def dot_nt(a, b):
    return lax.dot_general(a, b, (((1,), (1,)), ((), ())), preferred_element_type=F32)


def iota(shape, axis):
    return lax.broadcasted_iota(jnp.int32, shape, axis)


def routed(
    ids_ref,
    probs_ref,
    tokens_ref,
    cot_ref,
    gate_hbm,
    up_hbm,
    down_hbm,
    mixed_ref,
    grad_ref,
    xin,
    acts,
    gate_ref,
    up_ref,
    down_ref,
    out_box,
    in_box,
    home_box,
    back_box,
    back_hi,
    back_lo,
    spread,
    gather,
    part,
    first_in,
    second_out,
    second_in,
    load_sem,
    local_sem,
    send_sem,
    recv_sem,
    home_send,
    home_recv,
    ring_send,
    ring_recv,
    ready,
):
    x, e = lax.axis_index("dp"), lax.axis_index("expert")
    z, yc = e // 16, e % 16
    y, c = yc // 2, yc % 2
    right, left = lax.rem(x + 1, 4), lax.rem(x + 3, 4)
    opposite = lax.rem(x + 2, 4)
    sides = ((right, e), (left, e))
    near = (right, left)

    def plane(d, row):
        return (x, lax.rem(z + d, 8) * 16 + row)

    def greet(sem, device):
        pl.semaphore_signal(sem, inc=1, device_id=device, device_id_type=MESH)

    def push(src, dst, ssem, rsem, device):
        copy = pltpu.make_async_remote_copy(
            src_ref=src,
            dst_ref=dst,
            send_sem=ssem,
            recv_sem=rsem,
            device_id=device,
            device_id_type=MESH,
        )
        copy.start()
        return copy

    barrier = pltpu.get_barrier_semaphore()
    for side in sides:
        greet(barrier, side)
    for d in range(1, 8):
        greet(barrier, plane(d, yc))
    for i in range(1, 16):
        greet(barrier, plane(0, lax.rem(yc + i, 16)))
    loads = []
    for i, (src, dst) in enumerate(
        ((gate_hbm, gate_ref), (up_hbm, up_ref), (down_hbm, down_ref))
    ):
        load = pltpu.make_async_copy(src.at[0], dst, load_sem.at[i])
        load.start()
        loads.append(load)

    lane = iota((16, 128), 1)
    own_token = iota((16, 128), 0) == lane % 16
    ids = ids_ref[...].astype(F32)
    probs = probs_ref[...]
    rows = iota((128, 128), 0)
    cols = iota((128, 128), 1)
    turn = rows // 16
    step = jnp.where(turn % 2 == 1, (turn + 1) // 2, (8 - turn // 2) % 8)
    expert = ((z + step) % 8 * 16 + rows % 16).astype(F32)
    taken = jnp.zeros((128, 128), F32)
    weight = jnp.zeros((128, 128), F32)
    for k in range(8):
        id_row = jnp.sum(jnp.where(own_token, ids[:, k : k + 1], 0.0), axis=0, keepdims=True)
        prob_row = jnp.sum(
            jnp.where(own_token, probs[:, k : k + 1], 0.0), axis=0, keepdims=True
        )
        same = expert == id_row
        taken = jnp.where(same, 1.0, taken)
        weight = jnp.where(same, prob_row, weight)
    earlier = ((rows // 16 == cols // 16) & (rows < cols)).astype(F32).astype(BF16)
    rank = dot(taken.astype(BF16), earlier)
    code = jnp.where(taken > 0.0, (cols // 16 * 2).astype(F32) + rank, -1.0)
    feature = cols < 64
    out_value = jnp.where(feature, taken, weight)
    back_value = jnp.where(feature, weight, taken)
    out_high = out_value.astype(BF16).astype(F32)
    back_high = back_value.astype(BF16).astype(F32)
    out_low, back_low = out_value - out_high, back_value - back_high

    tokens = tokens_ref[...]
    cot = cot_ref[...]
    features = jnp.concatenate(
        [tokens[:, g * 128 : (g + 1) * 128] for g in range(4)]
        + [cot[:, g * 128 : (g + 1) * 128] for g in range(4)],
        axis=0,
    )
    slot = iota((16, 16, 128), 1).astype(F32)

    def expand(value, mine):
        full = jnp.where(mine, value[:, None, :], 0.0)
        return full.reshape(256, 128)

    for q in range(8):
        part_rows = slice(16 * q, 16 * (q + 1))
        mine = code[part_rows][:, None, :] == slot
        high = expand(out_high[part_rows], mine).astype(BF16)
        low = expand(out_low[part_rows], mine).astype(BF16)
        sent = dot(high, features) + dot(low, features)
        out_box[q] = sent.astype(BF16).reshape(16, 16, 128)

    pl.semaphore_wait(barrier, 24)
    for d in range(1, 8):
        greet(ready, plane(d, yc))
    keep = pltpu.make_async_copy(out_box.at[0, yc], in_box.at[0, yc], local_sem.at[0])
    keep.start()

    def send_to(q, i):
        row = lax.rem(yc + i, 16)
        k, j = q // (8 // CHUNKS), q % (8 // CHUNKS)
        push(
            out_box.at[q, row],
            in_box.at[k, j * 16 + yc],
            send_sem,
            recv_sem.at[k],
            plane(ORDER[q], row),
        )

    def send_group(q, first):
        def body(i, carry):
            send_to(q, i)
            return carry

        lax.fori_loop(first, 16, body, 0)

    send_group(0, 1)
    pl.semaphore_wait(ready, 7)
    for q in range(1, 8):
        send_group(q, 0)

    for q in range(8):
        part_rows = slice(16 * q, 16 * (q + 1))
        mine = code[part_rows][:, None, :] == slot
        high = expand(back_high[part_rows], mine)
        low = expand(back_low[part_rows], mine)
        back_hi[:, q * 256 : (q + 1) * 256] = high.T.astype(BF16)
        back_lo[:, q * 256 : (q + 1) * 256] = low.T.astype(BF16)
    big_row, big_col = iota((256, 256), 0), iota((256, 256), 1)
    gather[...] = (
        (big_row // 32 == big_col % 16 // 2)
        & (big_row % 32 // 2 == big_col // 16)
        & (big_row % 2 == big_col % 2)
    ).astype(F32).astype(BF16)
    spread[...] = (
        (big_col // 32 == big_row % 16 // 2)
        & (big_col % 32 // 2 == big_row // 16)
        & (big_row % 2 == big_col % 2)
    ).astype(F32).astype(BF16)
    for load in loads:
        load.wait()
    keep.wait()

    ring = {}

    def hop(stage, k, i, src, dst):
        ring[stage, k, i] = push(
            src, dst, ring_send.at[stage, k, i], ring_recv.at[stage, k, i], sides[i]
        )

    def halves(i):
        return pl.ds(HALF * i, HALF)

    def stage_partial(k):
        if k == 0:
            wait_bytes(in_box.at[0, pl.ds(0, SOURCES - 1)], recv_sem.at[0])
        else:
            wait_bytes(in_box.at[k], recv_sem.at[k])
        for a in range(SOURCES // 16):
            block = in_box[k, 16 * a : 16 * (a + 1)].reshape(256, 128)
            ordered = dot(gather[...], block).astype(BF16)
            for g in range(8):
                xin[k, 32 * a : 32 * (a + 1), g * 128 : (g + 1) * 128] = ordered[
                    32 * g : 32 * (g + 1)
                ]
        x_rows = xin[k, :, :COLUMNS]
        d_rows = xin[k, :, COLUMNS:]
        for n, (rows_in, ref) in enumerate(
            ((x_rows, gate_ref), (x_rows, up_ref), (d_rows, down_ref))
        ):
            value = dot_nt(rows_in, ref[...]).astype(BF16)
            part[k, :, :, n * FF : (n + 1) * FF] = value.reshape(4, PIECE, FF)
        for i in range(2):
            hop(0, k, i, part.at[k, opposite, :, halves(i)], first_in.at[k, :, halves(i)])

    def stage_sum(k):
        for i in range(2):
            ring[0, k, i].wait_recv()
        for i in range(2):
            span = slice(HALF * i, HALF * (i + 1))
            rest = slice(HALF * (1 - i), HALF * (2 - i))
            second_out[k, i, :, span] = (
                part[k, near[i], :, span].astype(F32) + first_in[k, :, span].astype(F32)
            ).astype(BF16)
            second_out[k, i, :, rest] = part[k, near[i], :, rest]
        for i in range(2):
            hop(1, k, i, second_out.at[k, i], second_in.at[k, i])

    def stage_act(k):
        for i in range(2):
            ring[1, k, i].wait_recv()

        def total(n):
            span = slice(n * FF, (n + 1) * FF)
            return (
                part[k, x, :, span].astype(F32)
                + second_in[k, 0, :, span].astype(F32)
                + second_in[k, 1, :, span].astype(F32)
            )

        gate, up, back = total(0), total(1), total(2)
        sig = jax.nn.sigmoid(gate)
        silu = gate * sig
        acts[k, x, :, :FF] = (silu * up).astype(BF16)
        acts[k, x, :, FF : 2 * FF] = (
            back * up * sig * (1.0 + gate * (1.0 - sig))
        ).astype(BF16)
        acts[k, x, :, 2 * FF :] = (back * silu).astype(BF16)
        for i in range(2):
            hop(2, k, i, acts.at[k, x], acts.at[k, x])

    def stage_forward(k):
        for i in range(2):
            ring[2, k, i].wait_recv()
        for i in range(2):
            piece = acts.at[k, near[1 - i], :, halves(i)]
            hop(3, k, i, piece, piece)

    def stage_home(k):
        for i in range(2):
            ring[3, k, i].wait_recv()
        h = acts[k].reshape(ROWS, WIDE)
        out = dot(h[:, :FF], down_ref[...]).astype(BF16)
        back = (
            dot(h[:, FF : 2 * FF], gate_ref[...]) + dot(h[:, 2 * FF :], up_ref[...])
        ).astype(BF16)
        for a in range(SOURCES // 16):
            span = slice(32 * a, 32 * (a + 1))
            stack = jnp.concatenate(
                [out[span, g * 128 : (g + 1) * 128] for g in range(4)]
                + [back[span, g * 128 : (g + 1) * 128] for g in range(4)],
                axis=0,
            )
            home_box[k, 16 * a : 16 * (a + 1)] = (
                dot(spread[...], stack).astype(BF16).reshape(16, 16, 128)
            )
        for j in range(8 // CHUNKS):
            q = k * (8 // CHUNKS) + j

            def body(i, carry, j=j, q=q):
                row = lax.rem(yc + i, 16)
                push(
                    home_box.at[k, j * 16 + row],
                    back_box.at[k, j * 16 + yc],
                    home_send,
                    home_recv.at[k],
                    plane(8 - ORDER[q], row),
                )
                return carry

            lax.fori_loop(1 if q == 0 else 0, 16, body, 0)
        if k == 0:
            copy = pltpu.make_async_copy(
                home_box.at[0, yc], back_box.at[0, yc], local_sem.at[1]
            )
            copy.start()
            ring["home"] = copy

    stages = (stage_partial, stage_sum, stage_act, stage_forward, stage_home)
    for t in range(CHUNKS + len(stages) - 1):
        for s in reversed(range(len(stages))):
            if 0 <= t - s < CHUNKS:
                stages[s](t - s)

    total = jnp.zeros((128, 128), F32)
    for k in range(CHUNKS):
        if k == 0:
            ring["home"].wait()
            wait_bytes(back_box.at[0, pl.ds(0, SOURCES - 1)], home_recv.at[0])
        else:
            wait_bytes(back_box.at[k], home_recv.at[k])
        block = back_box[k].reshape(SOURCES * 16, 128)
        span = slice(k * SOURCES * 16, (k + 1) * SOURCES * 16)
        total = total + dot(back_hi[:, span], block) + dot(back_lo[:, span], block)
    result = total.astype(BF16)
    for g in range(4):
        mixed_ref[:, g * 128 : (g + 1) * 128] = result[16 * g : 16 * (g + 1)]
        grad_ref[:, g * 128 : (g + 1) * 128] = result[64 + 16 * g : 64 + 16 * (g + 1)]

    for stage in range(4):
        for k in range(CHUNKS):
            for i in range(2):
                ring[stage, k, i].wait_send()
    wait_bytes(out_box.at[pl.ds(0, 7)], send_sem)
    wait_bytes(out_box.at[0, pl.ds(0, 15)], send_sem)
    wait_bytes(back_box.at[pl.ds(0, CHUNKS - 1)], home_send)
    wait_bytes(back_box.at[0, pl.ds(0, SOURCES - 1)], home_send)


def on_device(tokens, cotangent, expert_ids, gate_probs, w_gate, w_up, w_down):
    vmem = pl.BlockSpec(memory_space=pltpu.VMEM)
    hbm = pl.BlockSpec(memory_space=pl.ANY)

    def buf(*shape):
        return pltpu.VMEM(shape, BF16)

    dma = pltpu.SemaphoreType.DMA
    mixed, grad_tokens, xin, acts = pl.pallas_call(
        routed,
        out_shape=(
            jax.ShapeDtypeStruct((16, COLUMNS), BF16),
            jax.ShapeDtypeStruct((16, COLUMNS), BF16),
            jax.ShapeDtypeStruct((CHUNKS, ROWS, 2 * COLUMNS), BF16),
            jax.ShapeDtypeStruct((CHUNKS, 4, PIECE, WIDE), BF16),
        ),
        in_specs=[vmem] * 4 + [hbm] * 3,
        out_specs=(vmem, vmem, vmem, vmem),
        scratch_shapes=[
            buf(FF, COLUMNS),
            buf(FF, COLUMNS),
            buf(FF, COLUMNS),
            buf(8, 16, 16, 128),
            buf(CHUNKS, SOURCES, 16, 128),
            buf(CHUNKS, SOURCES, 16, 128),
            buf(CHUNKS, SOURCES, 16, 128),
            buf(128, 2048),
            buf(128, 2048),
            buf(256, 256),
            buf(256, 256),
            buf(CHUNKS, 4, PIECE, WIDE),
            buf(CHUNKS, PIECE, WIDE),
            buf(CHUNKS, 2, PIECE, WIDE),
            buf(CHUNKS, 2, PIECE, WIDE),
            dma((3,)),
            dma((2,)),
            dma,
            dma((CHUNKS,)),
            dma,
            dma((CHUNKS,)),
            dma((4, CHUNKS, 2)),
            dma((4, CHUNKS, 2)),
            pltpu.SemaphoreType.REGULAR,
        ],
        compiler_params=pltpu.CompilerParams(
            collective_id=0, has_side_effects=True, vmem_limit_bytes=60 * 1024 * 1024
        ),
    )(expert_ids, gate_probs, tokens, cotangent, w_gate, w_up, w_down)
    x_in = xin.reshape(256, 2 * COLUMNS)
    h = acts.reshape(256, WIDE)
    over_rows = (((0,), (0,)), ((), ()))

    def outer(a, b):
        return lax.dot_general(a, b, over_rows, preferred_element_type=F32).astype(BF16)[None]

    grad_gate = outer(h[:, FF : 2 * FF], x_in[:, :COLUMNS])
    grad_up = outer(h[:, 2 * FF :], x_in[:, :COLUMNS])
    grad_down = outer(h[:, :FF], x_in[:, COLUMNS:])
    return (mixed, grad_tokens, grad_gate, grad_up, grad_down)


def solution(mesh):
    in_specs = (
        P("expert", "dp"),
        P("expert", "dp"),
        P("expert", None),
        P("expert", None),
        P("expert", None, "dp"),
        P("expert", None, "dp"),
        P("expert", None, "dp"),
    )
    out_specs = (
        P("expert", "dp"),
        P("expert", "dp"),
        P("expert", None, "dp"),
        P("expert", None, "dp"),
        P("expert", None, "dp"),
    )
    return jax.shard_map(
        on_device, mesh=mesh, in_specs=in_specs, out_specs=out_specs, check_vma=False
    )
```

```python
import functools

import jax
import jax.numpy as jnp
from jax import lax
from jax.experimental import pallas as pl
from jax.experimental.pallas import tpu as pltpu
from jax.sharding import PartitionSpec as P

MESH = pl.DeviceIdType.MESH
BF16 = jnp.bfloat16
F32 = jnp.float32
CHUNKS = 4
SOURCES = 128 // CHUNKS
ROWS = 2 * SOURCES
PIECE = ROWS // 4
ORDER = (0, 1, 7, 2, 6, 3, 5, 4)
COLUMNS = 512
FF = 768
WIDE = 3 * FF
HALF = WIDE // 2


def wait_bytes(ref, sem):
    pltpu.make_async_copy(ref, ref, sem).wait()


def dot(a, b):
    return jnp.dot(a, b, preferred_element_type=F32)


def dot_nt(a, b):
    return lax.dot_general(a, b, (((1,), (1,)), ((), ())), preferred_element_type=F32)


def iota(shape, axis):
    return lax.broadcasted_iota(jnp.int32, shape, axis)


def routed(
    ids_hbm,
    probs_hbm,
    tokens_hbm,
    cot_hbm,
    gate_hbm,
    up_hbm,
    down_hbm,
    mixed_ref,
    grad_ref,
    grad_gate_ref,
    grad_up_ref,
    grad_down_ref,
    ids_ref,
    probs_ref,
    tokens_ref,
    cot_ref,
    xin,
    acts,
    gate_ref,
    up_ref,
    down_ref,
    out_box,
    in_box,
    home_box,
    back_box,
    back_hi,
    back_lo,
    spread,
    gather,
    part,
    first_in,
    second_out,
    second_in,
    load_sem,
    local_sem,
    send_sem,
    recv_sem,
    home_send,
    home_recv,
    ring_send,
    ring_recv,
    ready,
):
    x, e = lax.axis_index("dp"), lax.axis_index("expert")
    z, yc = e // 16, e % 16
    y, c = yc // 2, yc % 2
    right, left = lax.rem(x + 1, 4), lax.rem(x + 3, 4)
    opposite = lax.rem(x + 2, 4)
    sides = ((right, e), (left, e))
    near = (right, left)

    turned = [yc] + [lax.rem(yc + i, 16) for i in range(1, 16)]
    planes = [z * 16] + [lax.rem(z + d, 8) * 16 for d in range(1, 8)]

    def plane(d, row):
        return (x, planes[d % 8] + row)

    def greet(sem, device):
        pl.semaphore_signal(sem, inc=1, device_id=device, device_id_type=MESH)

    def push(src, dst, ssem, rsem, device):
        copy = pltpu.make_async_remote_copy(
            src_ref=src,
            dst_ref=dst,
            send_sem=ssem,
            recv_sem=rsem,
            device_id=device,
            device_id_type=MESH,
        )
        copy.start()
        return copy

    loads = []
    for i, (src, dst) in enumerate(
        (
            (ids_hbm, ids_ref),
            (probs_hbm, probs_ref),
            (tokens_hbm, tokens_ref),
            (cot_hbm, cot_ref),
            (gate_hbm.at[0], gate_ref),
            (up_hbm.at[0], up_ref),
            (down_hbm.at[0], down_ref),
        )
    ):
        load = pltpu.make_async_copy(src, dst, load_sem.at[i])
        load.start()
        loads.append(load)
    barrier = pltpu.get_barrier_semaphore()
    for side in sides:
        greet(barrier, side)
    for d in range(1, 8):
        greet(barrier, plane(d, yc))
    for i in range(1, 16):
        greet(barrier, plane(0, turned[i]))
    for load in loads[:4]:
        load.wait()
    own_token = (iota((16, 128), 0) == iota((16, 128), 1) % 16).astype(F32)

    def replicate(rows):
        return jnp.dot(
            rows, own_token, precision=lax.Precision.HIGHEST, preferred_element_type=F32
        )

    ids = replicate(ids_ref[...].astype(F32))
    probs = replicate(probs_ref[...])
    rows = iota((128, 128), 0)
    cols = iota((128, 128), 1)
    turn = rows // 16
    step = jnp.where(turn % 2 == 1, (turn + 1) // 2, (8 - turn // 2) % 8)
    expert = ((z + step) % 8 * 16 + rows % 16).astype(F32)
    taken = jnp.zeros((128, 128), F32)
    weight = jnp.zeros((128, 128), F32)
    for k in range(8):
        same = expert == ids[k : k + 1]
        taken = jnp.where(same, 1.0, taken)
        weight = jnp.where(same, probs[k : k + 1], weight)
    earlier = ((rows // 16 == cols // 16) & (rows < cols)).astype(F32).astype(BF16)
    rank = dot(taken.astype(BF16), earlier)
    code = jnp.where(taken > 0.0, (cols // 16 * 2).astype(F32) + rank, -1.0)
    feature = cols < 64
    out_value = jnp.where(feature, taken, weight)
    back_value = jnp.where(feature, weight, taken)
    out_high = out_value.astype(BF16).astype(F32)
    back_high = back_value.astype(BF16).astype(F32)
    out_low, back_low = out_value - out_high, back_value - back_high

    tokens = tokens_ref[...]
    cot = cot_ref[...]
    features = jnp.concatenate(
        [tokens[:, g * 128 : (g + 1) * 128] for g in range(4)]
        + [cot[:, g * 128 : (g + 1) * 128] for g in range(4)],
        axis=0,
    )
    slot = iota((16, 16, 128), 1).astype(F32)

    def expand(value, mine):
        full = jnp.where(mine, value[:, None, :], 0.0)
        return full.reshape(256, 128)

    def select(q):
        part_rows = slice(16 * q, 16 * (q + 1))
        mine = code[part_rows][:, None, :] == slot
        high = expand(out_high[part_rows], mine).astype(BF16)
        low = expand(out_low[part_rows], mine).astype(BF16)
        sent = dot(high, features) + dot(low, features)
        out_box[q] = sent.astype(BF16).reshape(16, 16, 128)

    def send_to(q, i):
        row = turned[i]
        k, j = q // (8 // CHUNKS), q % (8 // CHUNKS)
        push(
            out_box.at[q, row],
            in_box.at[k, j * 16 + yc],
            send_sem,
            recv_sem.at[k],
            plane(ORDER[q], row),
        )

    def send_group(q, first):
        for i in range(first, 16):
            send_to(q, i)

    select(0)
    pl.semaphore_wait(barrier, 24)
    for d in range(1, 8):
        greet(ready, plane(d, yc))
    keep = pltpu.make_async_copy(out_box.at[0, yc], in_box.at[0, yc], local_sem.at[0])
    keep.start()

    send_group(0, 1)
    select(1)
    pl.semaphore_wait(ready, 7)
    send_group(1, 0)
    for q in range(2, 8):
        select(q)
        send_group(q, 0)

    for q in range(8):
        part_rows = slice(16 * q, 16 * (q + 1))
        mine = code[part_rows][:, None, :] == slot
        high = expand(back_high[part_rows], mine)
        low = expand(back_low[part_rows], mine)
        back_hi[:, q * 256 : (q + 1) * 256] = high.T.astype(BF16)
        back_lo[:, q * 256 : (q + 1) * 256] = low.T.astype(BF16)
    big_row, big_col = iota((256, 256), 0), iota((256, 256), 1)
    gather[...] = (
        (big_row // 32 == big_col % 16 // 2)
        & (big_row % 32 // 2 == big_col // 16)
        & (big_row % 2 == big_col % 2)
    ).astype(F32).astype(BF16)
    spread[...] = (
        (big_col // 32 == big_row % 16 // 2)
        & (big_col % 32 // 2 == big_row // 16)
        & (big_row % 2 == big_col % 2)
    ).astype(F32).astype(BF16)
    for load in loads[4:]:
        load.wait()
    keep.wait()

    ring = {}

    def hop(stage, k, i, src, dst):
        ring[stage, k, i] = push(
            src, dst, ring_send.at[stage, k, i], ring_recv.at[stage, k, i], sides[i]
        )

    def halves(i):
        return pl.ds(HALF * i, HALF)

    def stage_partial(k):
        if k == 0:
            wait_bytes(in_box.at[0, pl.ds(0, SOURCES - 1)], recv_sem.at[0])
        else:
            wait_bytes(in_box.at[k], recv_sem.at[k])
        for a in range(SOURCES // 16):
            block = in_box[k, 16 * a : 16 * (a + 1)].reshape(256, 128)
            ordered = dot(gather[...], block).astype(BF16)
            for g in range(8):
                xin[k, 32 * a : 32 * (a + 1), g * 128 : (g + 1) * 128] = ordered[
                    32 * g : 32 * (g + 1)
                ]
        x_rows = xin[k, :, :COLUMNS]
        d_rows = xin[k, :, COLUMNS:]
        for n, (rows_in, ref) in enumerate(
            ((x_rows, gate_ref), (x_rows, up_ref), (d_rows, down_ref))
        ):
            value = dot_nt(rows_in, ref[...]).astype(BF16)
            part[k, :, :, n * FF : (n + 1) * FF] = value.reshape(4, PIECE, FF)
        for i in range(2):
            hop(0, k, i, part.at[k, opposite, :, halves(i)], first_in.at[k, :, halves(i)])

    def stage_sum(k):
        for i in range(2):
            ring[0, k, i].wait_recv()
        for i in range(2):
            span = slice(HALF * i, HALF * (i + 1))
            rest = slice(HALF * (1 - i), HALF * (2 - i))
            second_out[k, i, :, span] = (
                part[k, near[i], :, span].astype(F32) + first_in[k, :, span].astype(F32)
            ).astype(BF16)
            second_out[k, i, :, rest] = part[k, near[i], :, rest]
        for i in range(2):
            hop(1, k, i, second_out.at[k, i], second_in.at[k, i])

    def stage_act(k):
        for i in range(2):
            ring[1, k, i].wait_recv()

        def total(n):
            span = slice(n * FF, (n + 1) * FF)
            return (
                part[k, x, :, span].astype(F32)
                + second_in[k, 0, :, span].astype(F32)
                + second_in[k, 1, :, span].astype(F32)
            )

        gate, up, back = total(0), total(1), total(2)
        sig = jax.nn.sigmoid(gate)
        silu = gate * sig
        acts[k, x, :, :FF] = (silu * up).astype(BF16)
        acts[k, x, :, FF : 2 * FF] = (
            back * up * sig * (1.0 + gate * (1.0 - sig))
        ).astype(BF16)
        acts[k, x, :, 2 * FF :] = (back * silu).astype(BF16)
        for i in range(2):
            hop(2, k, i, acts.at[k, x], acts.at[k, x])

    def stage_forward(k):
        for i in range(2):
            ring[2, k, i].wait_recv()
        for i in range(2):
            piece = acts.at[k, near[1 - i], :, halves(i)]
            hop(3, k, i, piece, piece)

    def stage_home(k):
        for i in range(2):
            ring[3, k, i].wait_recv()
        h = acts[k].reshape(ROWS, WIDE)
        out = dot(h[:, :FF], down_ref[...]).astype(BF16)
        back = (
            dot(h[:, FF : 2 * FF], gate_ref[...]) + dot(h[:, 2 * FF :], up_ref[...])
        ).astype(BF16)
        for a in range(SOURCES // 16):
            span = slice(32 * a, 32 * (a + 1))
            stack = jnp.concatenate(
                [out[span, g * 128 : (g + 1) * 128] for g in range(4)]
                + [back[span, g * 128 : (g + 1) * 128] for g in range(4)],
                axis=0,
            )
            home_box[k, 16 * a : 16 * (a + 1)] = (
                dot(spread[...], stack).astype(BF16).reshape(16, 16, 128)
            )
        for j in range(8 // CHUNKS):
            q = k * (8 // CHUNKS) + j

            for i in range(1 if q == 0 else 0, 16):
                push(
                    home_box.at[k, j * 16 + turned[i]],
                    back_box.at[k, j * 16 + yc],
                    home_send,
                    home_recv.at[k],
                    plane(8 - ORDER[q], turned[i]),
                )
        if k == 0:
            copy = pltpu.make_async_copy(
                home_box.at[0, yc], back_box.at[0, yc], local_sem.at[1]
            )
            copy.start()
            ring["home"] = copy

    stages = (stage_partial, stage_sum, stage_act, stage_forward, stage_home)
    for t in range(CHUNKS + len(stages) - 1):
        for s in reversed(range(len(stages))):
            if 0 <= t - s < CHUNKS:
                stages[s](t - s)

    h_all = acts[...].reshape(256, WIDE)
    x_all = xin[...].reshape(256, 2 * COLUMNS)

    def outer(a, b):
        return lax.dot_general(
            a, b, (((0,), (0,)), ((), ())), preferred_element_type=F32
        ).astype(BF16)

    grad_gate_ref[...] = outer(h_all[:, FF : 2 * FF], x_all[:, :COLUMNS])
    grad_up_ref[...] = outer(h_all[:, 2 * FF :], x_all[:, :COLUMNS])
    grad_down_ref[...] = outer(h_all[:, :FF], x_all[:, COLUMNS:])

    total = jnp.zeros((128, 128), F32)
    for k in range(CHUNKS):
        if k == 0:
            ring["home"].wait()
            wait_bytes(back_box.at[0, pl.ds(0, SOURCES - 1)], home_recv.at[0])
        else:
            wait_bytes(back_box.at[k], home_recv.at[k])
        block = back_box[k].reshape(SOURCES * 16, 128)
        span = slice(k * SOURCES * 16, (k + 1) * SOURCES * 16)
        total = total + dot(back_hi[:, span], block) + dot(back_lo[:, span], block)
    result = total.astype(BF16)
    for g in range(4):
        mixed_ref[:, g * 128 : (g + 1) * 128] = result[16 * g : 16 * (g + 1)]
        grad_ref[:, g * 128 : (g + 1) * 128] = result[64 + 16 * g : 64 + 16 * (g + 1)]

    for stage in range(4):
        for k in range(CHUNKS):
            for i in range(2):
                ring[stage, k, i].wait_send()
    wait_bytes(out_box.at[pl.ds(0, 7)], send_sem)
    wait_bytes(out_box.at[0, pl.ds(0, 15)], send_sem)
    wait_bytes(back_box.at[pl.ds(0, CHUNKS - 1)], home_send)
    wait_bytes(back_box.at[0, pl.ds(0, SOURCES - 1)], home_send)


def store(*refs):
    sources, targets, sems = refs[:5], refs[5:10], refs[10]
    copies = [
        pltpu.make_async_copy(src, dst, sems.at[i])
        for i, (src, dst) in enumerate(zip(sources, targets))
    ]
    for copy in copies:
        copy.start()
    for copy in copies:
        copy.wait()


def on_device(tokens, cotangent, expert_ids, gate_probs, w_gate, w_up, w_down):
    vmem = pl.BlockSpec(memory_space=pltpu.VMEM)
    hbm = pl.BlockSpec(memory_space=pl.ANY)
    far = pl.BlockSpec(memory_space=pltpu.MemorySpace.HBM)

    def buf(*shape):
        return pltpu.VMEM(shape, BF16)

    dma = pltpu.SemaphoreType.DMA
    results = pl.pallas_call(
        routed,
        out_shape=(
            jax.ShapeDtypeStruct((16, COLUMNS), BF16),
            jax.ShapeDtypeStruct((16, COLUMNS), BF16),
            jax.ShapeDtypeStruct((FF, COLUMNS), BF16),
            jax.ShapeDtypeStruct((FF, COLUMNS), BF16),
            jax.ShapeDtypeStruct((FF, COLUMNS), BF16),
        ),
        in_specs=[far] * 7,
        out_specs=(vmem,) * 5,
        scratch_shapes=[
            pltpu.VMEM((8, 16), jnp.int32),
            pltpu.VMEM((8, 16), F32),
            buf(16, COLUMNS),
            buf(16, COLUMNS),
            buf(CHUNKS, ROWS, 2 * COLUMNS),
            buf(CHUNKS, 4, PIECE, WIDE),
            buf(FF, COLUMNS),
            buf(FF, COLUMNS),
            buf(FF, COLUMNS),
            buf(8, 16, 16, 128),
            buf(CHUNKS, SOURCES, 16, 128),
            buf(CHUNKS, SOURCES, 16, 128),
            buf(CHUNKS, SOURCES, 16, 128),
            buf(128, 2048),
            buf(128, 2048),
            buf(256, 256),
            buf(256, 256),
            buf(CHUNKS, 4, PIECE, WIDE),
            buf(CHUNKS, PIECE, WIDE),
            buf(CHUNKS, 2, PIECE, WIDE),
            buf(CHUNKS, 2, PIECE, WIDE),
            dma((7,)),
            dma((2,)),
            dma,
            dma((CHUNKS,)),
            dma,
            dma((CHUNKS,)),
            dma((4, CHUNKS, 2)),
            dma((4, CHUNKS, 2)),
            pltpu.SemaphoreType.REGULAR,
        ],
        compiler_params=pltpu.CompilerParams(
            collective_id=0, has_side_effects=True, vmem_limit_bytes=51 * 1024 * 1024
        ),
    )(*[pltpu.with_memory_space_constraint(a, pltpu.MemorySpace.HBM) for a in (expert_ids.T, gate_probs.T, tokens, cotangent, w_gate, w_up, w_down)])
    shapes = [jax.ShapeDtypeStruct(r.shape, r.dtype) for r in results]
    mixed, grad_tokens, grad_gate, grad_up, grad_down = pl.pallas_call(
        store,
        out_shape=shapes,
        in_specs=[vmem] * 5,
        out_specs=[hbm] * 5,
        scratch_shapes=[dma((5,))],
        compiler_params=pltpu.CompilerParams(vmem_limit_bytes=4 * 1024 * 1024),
    )(*results)
    return (mixed, grad_tokens, grad_gate[None], grad_up[None], grad_down[None])


def solution(mesh):
    in_specs = (
        P("expert", "dp"),
        P("expert", "dp"),
        P("expert", None),
        P("expert", None),
        P("expert", None, "dp"),
        P("expert", None, "dp"),
        P("expert", None, "dp"),
    )
    out_specs = (
        P("expert", "dp"),
        P("expert", "dp"),
        P("expert", None, "dp"),
        P("expert", None, "dp"),
        P("expert", None, "dp"),
    )
    return jax.shard_map(
        on_device, mesh=mesh, in_specs=in_specs, out_specs=out_specs, check_vma=False
    )
```

```python
import functools

import jax
import jax.numpy as jnp
from jax import lax
from jax.experimental import pallas as pl
from jax.experimental.pallas import tpu as pltpu
from jax.sharding import PartitionSpec as P

MESH = pl.DeviceIdType.MESH
BF16 = jnp.bfloat16
F32 = jnp.float32
CHUNKS = 4
SOURCES = 128 // CHUNKS
ROWS = 2 * SOURCES
PIECE = ROWS // 4
ORDER = (0, 1, 7, 2, 6, 3, 5, 4)
COLUMNS = 512
FF = 768
WIDE = 3 * FF
HALF = WIDE // 2


def wait_bytes(ref, sem):
    pltpu.make_async_copy(ref, ref, sem).wait()


def dot(a, b):
    return jnp.dot(a, b, preferred_element_type=F32)


def dot_nt(a, b):
    return lax.dot_general(a, b, (((1,), (1,)), ((), ())), preferred_element_type=F32)


def iota(shape, axis):
    return lax.broadcasted_iota(jnp.int32, shape, axis)


def routed(
    ids_hbm,
    probs_hbm,
    tokens_hbm,
    cot_hbm,
    gate_hbm,
    up_hbm,
    down_hbm,
    mixed_ref,
    grad_ref,
    grad_gate_ref,
    grad_up_ref,
    grad_down_ref,
    ids_ref,
    probs_ref,
    tokens_ref,
    cot_ref,
    xin,
    acts,
    gate_ref,
    up_ref,
    down_ref,
    out_box,
    in_box,
    home_box,
    back_box,
    back_hi,
    back_lo,
    spread,
    gather,
    part,
    first_in,
    second_out,
    second_in,
    load_sem,
    local_sem,
    send_sem,
    recv_sem,
    home_send,
    home_recv,
    ring_send,
    ring_recv,
    ready,
):
    x, e = lax.axis_index("dp"), lax.axis_index("expert")
    z, yc = e // 16, e % 16
    y, c = yc // 2, yc % 2
    right, left = lax.rem(x + 1, 4), lax.rem(x + 3, 4)
    opposite = lax.rem(x + 2, 4)
    sides = ((right, e), (left, e))
    near = (right, left)

    turned = [yc] + [lax.rem(yc + i, 16) for i in range(1, 16)]
    planes = [z * 16] + [lax.rem(z + d, 8) * 16 for d in range(1, 8)]

    def plane(d, row):
        return (x, planes[d % 8] + row)

    def greet(sem, device):
        pl.semaphore_signal(sem, inc=1, device_id=device, device_id_type=MESH)

    def push(src, dst, ssem, rsem, device):
        copy = pltpu.make_async_remote_copy(
            src_ref=src,
            dst_ref=dst,
            send_sem=ssem,
            recv_sem=rsem,
            device_id=device,
            device_id_type=MESH,
        )
        copy.start()
        return copy

    loads = []
    for i, (src, dst) in enumerate(
        (
            (ids_hbm, ids_ref),
            (probs_hbm, probs_ref),
            (tokens_hbm, tokens_ref),
            (cot_hbm, cot_ref),
            (gate_hbm.at[0], gate_ref),
            (up_hbm.at[0], up_ref),
            (down_hbm.at[0], down_ref),
        )
    ):
        load = pltpu.make_async_copy(src, dst, load_sem.at[i])
        load.start()
        loads.append(load)
    barrier = pltpu.get_barrier_semaphore()
    for side in sides:
        greet(barrier, side)
    for d in range(1, 8):
        greet(barrier, plane(d, yc))
    for i in range(1, 16):
        greet(barrier, plane(0, turned[i]))
    for load in loads[:4]:
        load.wait()
    own_token = (iota((16, 128), 0) == iota((16, 128), 1) % 16).astype(F32)

    def replicate(rows):
        return jnp.dot(
            rows, own_token, precision=lax.Precision.HIGHEST, preferred_element_type=F32
        )

    ids = replicate(ids_ref[...].astype(F32))
    probs = replicate(probs_ref[...])
    rows = iota((128, 128), 0)
    cols = iota((128, 128), 1)
    turn = rows // 16
    step = jnp.where(turn % 2 == 1, (turn + 1) // 2, (8 - turn // 2) % 8)
    expert = ((z + step) % 8 * 16 + rows % 16).astype(F32)
    taken = jnp.zeros((128, 128), F32)
    weight = jnp.zeros((128, 128), F32)
    for k in range(8):
        same = expert == ids[k : k + 1]
        taken = jnp.where(same, 1.0, taken)
        weight = jnp.where(same, probs[k : k + 1], weight)
    earlier = ((rows // 16 == cols // 16) & (rows < cols)).astype(F32).astype(BF16)
    rank = dot(taken.astype(BF16), earlier)
    code = jnp.where(taken > 0.0, (cols // 16 * 2).astype(F32) + rank, -1.0)
    feature = cols < 64
    out_value = jnp.where(feature, taken, weight)
    back_value = jnp.where(feature, weight, taken)
    out_high = out_value.astype(BF16).astype(F32)
    back_high = back_value.astype(BF16).astype(F32)
    out_low, back_low = out_value - out_high, back_value - back_high

    tokens = tokens_ref[...]
    cot = cot_ref[...]
    features = jnp.concatenate(
        [tokens[:, g * 128 : (g + 1) * 128] for g in range(4)]
        + [cot[:, g * 128 : (g + 1) * 128] for g in range(4)],
        axis=0,
    )
    slot = iota((16, 16, 128), 1).astype(F32)

    def expand(value, mine):
        full = jnp.where(mine, value[:, None, :], 0.0)
        return full.reshape(256, 128)

    def select(q):
        part_rows = slice(16 * q, 16 * (q + 1))
        mine = code[part_rows][:, None, :] == slot
        high = expand(out_high[part_rows], mine).astype(BF16)
        low = expand(out_low[part_rows], mine).astype(BF16)
        sent = dot(high, features) + dot(low, features)
        out_box[q] = sent.astype(BF16).reshape(16, 16, 128)

    def send_to(q, i):
        row = turned[i]
        k, j = q // (8 // CHUNKS), q % (8 // CHUNKS)
        push(
            out_box.at[q, row],
            in_box.at[k, j * 16 + yc],
            send_sem,
            recv_sem.at[k],
            plane(ORDER[q], row),
        )

    def send_group(q, first):
        for i in range(first, 16):
            send_to(q, i)

    select(0)
    pl.semaphore_wait(barrier, 24)
    for d in range(1, 8):
        greet(ready.at[8 - d], plane(d, yc))
    keep = pltpu.make_async_copy(out_box.at[0, yc], in_box.at[0, yc], local_sem.at[0])
    keep.start()

    send_group(0, 1)
    for q in range(1, 8):
        select(q)
        pl.semaphore_wait(ready.at[ORDER[q]], 1)
        send_group(q, 0)

    for q in range(8):
        part_rows = slice(16 * q, 16 * (q + 1))
        mine = code[part_rows][:, None, :] == slot
        high = expand(back_high[part_rows], mine)
        low = expand(back_low[part_rows], mine)
        back_hi[:, q * 256 : (q + 1) * 256] = high.T.astype(BF16)
        back_lo[:, q * 256 : (q + 1) * 256] = low.T.astype(BF16)
    big_row, big_col = iota((256, 256), 0), iota((256, 256), 1)
    gather[...] = (
        (big_row // 32 == big_col % 16 // 2)
        & (big_row % 32 // 2 == big_col // 16)
        & (big_row % 2 == big_col % 2)
    ).astype(F32).astype(BF16)
    spread[...] = (
        (big_col // 32 == big_row % 16 // 2)
        & (big_col % 32 // 2 == big_row // 16)
        & (big_row % 2 == big_col % 2)
    ).astype(F32).astype(BF16)
    for load in loads[4:]:
        load.wait()
    keep.wait()

    ring = {}

    def hop(stage, k, i, src, dst):
        ring[stage, k, i] = push(
            src, dst, ring_send.at[stage, k, i], ring_recv.at[stage, k, i], sides[i]
        )

    def halves(i):
        return pl.ds(HALF * i, HALF)

    def stage_partial(k):
        if k == 0:
            wait_bytes(in_box.at[0, pl.ds(0, SOURCES - 1)], recv_sem.at[0])
        else:
            wait_bytes(in_box.at[k], recv_sem.at[k])
        for a in range(SOURCES // 16):
            block = in_box[k, 16 * a : 16 * (a + 1)].reshape(256, 128)
            ordered = dot(gather[...], block).astype(BF16)
            for g in range(8):
                xin[k, 32 * a : 32 * (a + 1), g * 128 : (g + 1) * 128] = ordered[
                    32 * g : 32 * (g + 1)
                ]
        x_rows = xin[k, :, :COLUMNS]
        d_rows = xin[k, :, COLUMNS:]
        for n, (rows_in, ref) in enumerate(
            ((x_rows, gate_ref), (x_rows, up_ref), (d_rows, down_ref))
        ):
            value = dot_nt(rows_in, ref[...]).astype(BF16)
            part[k, :, :, n * FF : (n + 1) * FF] = value.reshape(4, PIECE, FF)
        for i in range(2):
            hop(0, k, i, part.at[k, opposite, :, halves(i)], first_in.at[k, :, halves(i)])

    def stage_sum(k):
        for i in range(2):
            ring[0, k, i].wait_recv()
        for i in range(2):
            span = slice(HALF * i, HALF * (i + 1))
            rest = slice(HALF * (1 - i), HALF * (2 - i))
            second_out[k, i, :, span] = (
                part[k, near[i], :, span].astype(F32) + first_in[k, :, span].astype(F32)
            ).astype(BF16)
            second_out[k, i, :, rest] = part[k, near[i], :, rest]
        for i in range(2):
            hop(1, k, i, second_out.at[k, i], second_in.at[k, i])

    def stage_act(k):
        for i in range(2):
            ring[1, k, i].wait_recv()

        def total(n):
            span = slice(n * FF, (n + 1) * FF)
            return (
                part[k, x, :, span].astype(F32)
                + second_in[k, 0, :, span].astype(F32)
                + second_in[k, 1, :, span].astype(F32)
            )

        gate, up, back = total(0), total(1), total(2)
        sig = jax.nn.sigmoid(gate)
        silu = gate * sig
        acts[k, x, :, :FF] = (silu * up).astype(BF16)
        acts[k, x, :, FF : 2 * FF] = (
            back * up * sig * (1.0 + gate * (1.0 - sig))
        ).astype(BF16)
        acts[k, x, :, 2 * FF :] = (back * silu).astype(BF16)
        for i in range(2):
            hop(2, k, i, acts.at[k, x], acts.at[k, x])

    def stage_forward(k):
        for i in range(2):
            ring[2, k, i].wait_recv()
        for i in range(2):
            piece = acts.at[k, near[1 - i], :, halves(i)]
            hop(3, k, i, piece, piece)

    def stage_home(k):
        for i in range(2):
            ring[3, k, i].wait_recv()
        h = acts[k].reshape(ROWS, WIDE)
        out = dot(h[:, :FF], down_ref[...]).astype(BF16)
        back = (
            dot(h[:, FF : 2 * FF], gate_ref[...]) + dot(h[:, 2 * FF :], up_ref[...])
        ).astype(BF16)
        for a in range(SOURCES // 16):
            span = slice(32 * a, 32 * (a + 1))
            stack = jnp.concatenate(
                [out[span, g * 128 : (g + 1) * 128] for g in range(4)]
                + [back[span, g * 128 : (g + 1) * 128] for g in range(4)],
                axis=0,
            )
            home_box[k, 16 * a : 16 * (a + 1)] = (
                dot(spread[...], stack).astype(BF16).reshape(16, 16, 128)
            )
        for j in range(8 // CHUNKS):
            q = k * (8 // CHUNKS) + j

            for i in range(1 if q == 0 else 0, 16):
                push(
                    home_box.at[k, j * 16 + turned[i]],
                    back_box.at[k, j * 16 + yc],
                    home_send,
                    home_recv.at[k],
                    plane(8 - ORDER[q], turned[i]),
                )
        if k == 0:
            copy = pltpu.make_async_copy(
                home_box.at[0, yc], back_box.at[0, yc], local_sem.at[1]
            )
            copy.start()
            ring["home"] = copy

    stages = (stage_partial, stage_sum, stage_act, stage_forward, stage_home)
    for t in range(CHUNKS + len(stages) - 1):
        for s in range(len(stages)):
            if 0 <= t - s < CHUNKS:
                stages[s](t - s)

    h_all = acts[...].reshape(256, WIDE)
    x_all = xin[...].reshape(256, 2 * COLUMNS)

    def outer(a, b):
        return lax.dot_general(
            a, b, (((0,), (0,)), ((), ())), preferred_element_type=F32
        ).astype(BF16)

    grad_gate_ref[...] = outer(h_all[:, FF : 2 * FF], x_all[:, :COLUMNS])
    grad_up_ref[...] = outer(h_all[:, 2 * FF :], x_all[:, :COLUMNS])
    grad_down_ref[...] = outer(h_all[:, :FF], x_all[:, COLUMNS:])

    total = jnp.zeros((128, 128), F32)
    for k in range(CHUNKS):
        if k == 0:
            ring["home"].wait()
            wait_bytes(back_box.at[0, pl.ds(0, SOURCES - 1)], home_recv.at[0])
        else:
            wait_bytes(back_box.at[k], home_recv.at[k])
        block = back_box[k].reshape(SOURCES * 16, 128)
        span = slice(k * SOURCES * 16, (k + 1) * SOURCES * 16)
        total = total + dot(back_hi[:, span], block) + dot(back_lo[:, span], block)
    result = total.astype(BF16)
    for g in range(4):
        mixed_ref[:, g * 128 : (g + 1) * 128] = result[16 * g : 16 * (g + 1)]
        grad_ref[:, g * 128 : (g + 1) * 128] = result[64 + 16 * g : 64 + 16 * (g + 1)]

    for stage in range(4):
        for k in range(CHUNKS):
            for i in range(2):
                ring[stage, k, i].wait_send()
    wait_bytes(out_box.at[pl.ds(0, 7)], send_sem)
    wait_bytes(out_box.at[0, pl.ds(0, 15)], send_sem)
    wait_bytes(back_box.at[pl.ds(0, CHUNKS - 1)], home_send)
    wait_bytes(back_box.at[0, pl.ds(0, SOURCES - 1)], home_send)


def store(*refs):
    sources, targets, sems = refs[:5], refs[5:10], refs[10]
    copies = [
        pltpu.make_async_copy(src, dst, sems.at[i])
        for i, (src, dst) in enumerate(zip(sources, targets))
    ]
    for copy in copies:
        copy.start()
    for copy in copies:
        copy.wait()


def on_device(tokens, cotangent, expert_ids, gate_probs, w_gate, w_up, w_down):
    vmem = pl.BlockSpec(memory_space=pltpu.VMEM)
    hbm = pl.BlockSpec(memory_space=pl.ANY)
    far = pl.BlockSpec(memory_space=pltpu.MemorySpace.HBM)

    def buf(*shape):
        return pltpu.VMEM(shape, BF16)

    dma = pltpu.SemaphoreType.DMA
    results = pl.pallas_call(
        routed,
        out_shape=(
            jax.ShapeDtypeStruct((16, COLUMNS), BF16),
            jax.ShapeDtypeStruct((16, COLUMNS), BF16),
            jax.ShapeDtypeStruct((FF, COLUMNS), BF16),
            jax.ShapeDtypeStruct((FF, COLUMNS), BF16),
            jax.ShapeDtypeStruct((FF, COLUMNS), BF16),
        ),
        in_specs=[far] * 7,
        out_specs=(vmem,) * 5,
        scratch_shapes=[
            pltpu.VMEM((8, 16), jnp.int32),
            pltpu.VMEM((8, 16), F32),
            buf(16, COLUMNS),
            buf(16, COLUMNS),
            buf(CHUNKS, ROWS, 2 * COLUMNS),
            buf(CHUNKS, 4, PIECE, WIDE),
            buf(FF, COLUMNS),
            buf(FF, COLUMNS),
            buf(FF, COLUMNS),
            buf(8, 16, 16, 128),
            buf(CHUNKS, SOURCES, 16, 128),
            buf(CHUNKS, SOURCES, 16, 128),
            buf(CHUNKS, SOURCES, 16, 128),
            buf(128, 2048),
            buf(128, 2048),
            buf(256, 256),
            buf(256, 256),
            buf(CHUNKS, 4, PIECE, WIDE),
            buf(CHUNKS, PIECE, WIDE),
            buf(CHUNKS, 2, PIECE, WIDE),
            buf(CHUNKS, 2, PIECE, WIDE),
            dma((7,)),
            dma((2,)),
            dma,
            dma((CHUNKS,)),
            dma,
            dma((CHUNKS,)),
            dma((4, CHUNKS, 2)),
            dma((4, CHUNKS, 2)),
            pltpu.SemaphoreType.REGULAR((8,)),
        ],
        compiler_params=pltpu.CompilerParams(
            collective_id=0, has_side_effects=True, vmem_limit_bytes=51 * 1024 * 1024
        ),
    )(*[pltpu.with_memory_space_constraint(a, pltpu.MemorySpace.HBM) for a in (expert_ids.T, gate_probs.T, tokens, cotangent, w_gate, w_up, w_down)])
    shapes = [jax.ShapeDtypeStruct(r.shape, r.dtype) for r in results]
    mixed, grad_tokens, grad_gate, grad_up, grad_down = pl.pallas_call(
        store,
        out_shape=shapes,
        in_specs=[vmem] * 5,
        out_specs=[hbm] * 5,
        scratch_shapes=[dma((5,))],
        compiler_params=pltpu.CompilerParams(vmem_limit_bytes=4 * 1024 * 1024),
    )(*results)
    return (mixed, grad_tokens, grad_gate[None], grad_up[None], grad_down[None])


def solution(mesh):
    in_specs = (
        P("expert", "dp"),
        P("expert", "dp"),
        P("expert", None),
        P("expert", None),
        P("expert", None, "dp"),
        P("expert", None, "dp"),
        P("expert", None, "dp"),
    )
    out_specs = (
        P("expert", "dp"),
        P("expert", "dp"),
        P("expert", None, "dp"),
        P("expert", None, "dp"),
        P("expert", None, "dp"),
    )
    return jax.shard_map(
        on_device, mesh=mesh, in_specs=in_specs, out_specs=out_specs, check_vma=False
    )
```

```python
import functools

import jax
import jax.numpy as jnp
from jax import lax
from jax.experimental import pallas as pl
from jax.experimental.pallas import tpu as pltpu
from jax.sharding import PartitionSpec as P

MESH = pl.DeviceIdType.MESH
BF16 = jnp.bfloat16
F32 = jnp.float32
CHUNKS = 4
SOURCES = 128 // CHUNKS
ROWS = 2 * SOURCES
PIECE = ROWS // 4
ORDER = (0, 1, 7, 2, 6, 3, 5, 4)
COLUMNS = 512
FF = 768
WIDE = 3 * FF
HALF = WIDE // 2


def wait_bytes(ref, sem):
    pltpu.make_async_copy(ref, ref, sem).wait()


def dot(a, b):
    return jnp.dot(a, b, preferred_element_type=F32)


def dot_nt(a, b):
    return lax.dot_general(a, b, (((1,), (1,)), ((), ())), preferred_element_type=F32)


def iota(shape, axis):
    return lax.broadcasted_iota(jnp.int32, shape, axis)


def routed(
    ids_hbm,
    probs_hbm,
    tokens_hbm,
    cot_hbm,
    gate_hbm,
    up_hbm,
    down_hbm,
    mixed_ref,
    grad_ref,
    grad_gate_ref,
    grad_up_ref,
    grad_down_ref,
    ids_ref,
    probs_ref,
    tokens_ref,
    cot_ref,
    xin,
    acts,
    gate_ref,
    up_ref,
    down_ref,
    out_box,
    in_box,
    home_box,
    back_box,
    back_hi,
    back_lo,
    spread,
    gather,
    part,
    first_in,
    second_out,
    second_in,
    load_sem,
    local_sem,
    send_sem,
    recv_sem,
    home_send,
    home_recv,
    ring_send,
    ring_recv,
    ready,
):
    x, e = lax.axis_index("dp"), lax.axis_index("expert")
    z, yc = e // 16, e % 16
    y, c = yc // 2, yc % 2
    right, left = lax.rem(x + 1, 4), lax.rem(x + 3, 4)
    opposite = lax.rem(x + 2, 4)
    sides = ((right, e), (left, e))
    near = (right, left)

    turned = [yc] + [lax.rem(yc + i, 16) for i in range(1, 16)]
    planes = [z * 16] + [lax.rem(z + d, 8) * 16 for d in range(1, 8)]

    def plane(d, row):
        return (x, planes[d % 8] + row)

    def greet(sem, device):
        pl.semaphore_signal(sem, inc=1, device_id=device, device_id_type=MESH)

    def push(src, dst, ssem, rsem, device):
        copy = pltpu.make_async_remote_copy(
            src_ref=src,
            dst_ref=dst,
            send_sem=ssem,
            recv_sem=rsem,
            device_id=device,
            device_id_type=MESH,
        )
        copy.start()
        return copy

    loads = []
    for i, (src, dst) in enumerate(
        (
            (ids_hbm, ids_ref),
            (probs_hbm, probs_ref),
            (tokens_hbm, tokens_ref),
            (cot_hbm, cot_ref),
            (gate_hbm.at[0], gate_ref),
            (up_hbm.at[0], up_ref),
            (down_hbm.at[0], down_ref),
        )
    ):
        load = pltpu.make_async_copy(src, dst, load_sem.at[i])
        load.start()
        loads.append(load)
    barrier = pltpu.get_barrier_semaphore()
    for side in sides:
        greet(barrier, side)
    for d in range(1, 8):
        greet(barrier, plane(d, yc))
    for i in range(1, 16):
        greet(barrier, plane(0, turned[i]))
    for load in loads[:4]:
        load.wait()
    own_token = (iota((16, 128), 0) == iota((16, 128), 1) % 16).astype(F32)

    def replicate(rows):
        return jnp.dot(
            rows, own_token, precision=lax.Precision.HIGHEST, preferred_element_type=F32
        )

    ids = replicate(ids_ref[...].astype(F32))
    probs = replicate(probs_ref[...])
    rows = iota((128, 128), 0)
    cols = iota((128, 128), 1)
    turn = rows // 16
    step = jnp.where(turn % 2 == 1, (turn + 1) // 2, (8 - turn // 2) % 8)
    expert = ((z + step) % 8 * 16 + rows % 16).astype(F32)
    taken = jnp.zeros((128, 128), F32)
    weight = jnp.zeros((128, 128), F32)
    for k in range(8):
        same = expert == ids[k : k + 1]
        taken = jnp.where(same, 1.0, taken)
        weight = jnp.where(same, probs[k : k + 1], weight)
    earlier = ((rows // 16 == cols // 16) & (rows < cols)).astype(F32).astype(BF16)
    rank = dot(taken.astype(BF16), earlier)
    code = jnp.where(taken > 0.0, (cols // 16 * 2).astype(F32) + rank, -1.0)
    feature = cols < 64
    out_value = jnp.where(feature, taken, weight)
    back_value = jnp.where(feature, weight, taken)
    out_high = out_value.astype(BF16).astype(F32)
    back_high = back_value.astype(BF16).astype(F32)
    out_low, back_low = out_value - out_high, back_value - back_high

    tokens = tokens_ref[...]
    cot = cot_ref[...]
    features = jnp.concatenate(
        [tokens[:, g * 128 : (g + 1) * 128] for g in range(4)]
        + [cot[:, g * 128 : (g + 1) * 128] for g in range(4)],
        axis=0,
    )
    slot = iota((16, 16, 128), 1).astype(F32)

    def expand(value, mine):
        full = jnp.where(mine, value[:, None, :], 0.0)
        return full.reshape(256, 128)

    def select(q):
        part_rows = slice(16 * q, 16 * (q + 1))
        mine = code[part_rows][:, None, :] == slot
        high = expand(out_high[part_rows], mine).astype(BF16)
        low = expand(out_low[part_rows], mine).astype(BF16)
        sent = dot(high, features) + dot(low, features)
        out_box[q] = sent.astype(BF16).reshape(16, 16, 128)

    def send_to(q, i):
        row = turned[i]
        k, j = q // (8 // CHUNKS), q % (8 // CHUNKS)
        push(
            out_box.at[q, row],
            in_box.at[k, j * 16 + yc],
            send_sem,
            recv_sem.at[k],
            plane(ORDER[q], row),
        )

    def send_group(q, first):
        for i in range(first, 16):
            send_to(q, i)

    select(0)
    pl.semaphore_wait(barrier, 24)
    for d in range(1, 8):
        greet(ready.at[8 - d], plane(d, yc))
    keep = pltpu.make_async_copy(out_box.at[0, yc], in_box.at[0, yc], local_sem.at[0])
    keep.start()

    send_group(0, 1)
    for q in range(1, 8):
        select(q)
        pl.semaphore_wait(ready.at[ORDER[q]], 1)
        send_group(q, 0)

    def weigh(q):
        part_rows = slice(16 * q, 16 * (q + 1))
        mine = code[part_rows][:, None, :] == slot
        high = expand(back_high[part_rows], mine)
        low = expand(back_low[part_rows], mine)
        back_hi[:, q * 256 : (q + 1) * 256] = high.T.astype(BF16)
        back_lo[:, q * 256 : (q + 1) * 256] = low.T.astype(BF16)

    big_row, big_col = iota((256, 256), 0), iota((256, 256), 1)
    gather[...] = (
        (big_row // 32 == big_col % 16 // 2)
        & (big_row % 32 // 2 == big_col // 16)
        & (big_row % 2 == big_col % 2)
    ).astype(F32).astype(BF16)
    spread[...] = (
        (big_col // 32 == big_row % 16 // 2)
        & (big_col % 32 // 2 == big_row // 16)
        & (big_row % 2 == big_col % 2)
    ).astype(F32).astype(BF16)
    for load in loads[4:]:
        load.wait()
    keep.wait()

    ring = {}

    def hop(stage, k, i, src, dst):
        ring[stage, k, i] = push(
            src, dst, ring_send.at[stage, k, i], ring_recv.at[stage, k, i], sides[i]
        )

    def halves(i):
        return pl.ds(HALF * i, HALF)

    def stage_partial(k):
        if k == 0:
            wait_bytes(in_box.at[0, pl.ds(0, SOURCES - 1)], recv_sem.at[0])
        else:
            wait_bytes(in_box.at[k], recv_sem.at[k])
        for a in range(SOURCES // 16):
            block = in_box[k, 16 * a : 16 * (a + 1)].reshape(256, 128)
            ordered = dot(gather[...], block).astype(BF16)
            for g in range(8):
                xin[k, 32 * a : 32 * (a + 1), g * 128 : (g + 1) * 128] = ordered[
                    32 * g : 32 * (g + 1)
                ]
        x_rows = xin[k, :, :COLUMNS]
        d_rows = xin[k, :, COLUMNS:]
        for n, (rows_in, ref) in enumerate(
            ((x_rows, gate_ref), (x_rows, up_ref), (d_rows, down_ref))
        ):
            value = dot_nt(rows_in, ref[...]).astype(BF16)
            part[k, :, :, n * FF : (n + 1) * FF] = value.reshape(4, PIECE, FF)
        for i in range(2):
            hop(0, k, i, part.at[k, opposite, :, halves(i)], first_in.at[k, :, halves(i)])
        for i in range(2):
            other = halves(1 - i)
            hop(4, k, i, part.at[k, near[i], :, other], second_in.at[k, i, :, other])

    def stage_sum(k):
        for i in range(2):
            ring[0, k, i].wait_recv()
        for i in range(2):
            span = slice(HALF * i, HALF * (i + 1))
            second_out[k, i] = (
                part[k, near[i], :, span].astype(F32) + first_in[k, :, span].astype(F32)
            ).astype(BF16)
        for i in range(2):
            hop(1, k, i, second_out.at[k, i], second_in.at[k, i, :, halves(i)])

    def stage_act(k):
        for i in range(2):
            ring[4, k, i].wait_recv()
            ring[1, k, i].wait_recv()

        def total(n):
            span = slice(n * FF, (n + 1) * FF)
            return (
                part[k, x, :, span].astype(F32)
                + second_in[k, 0, :, span].astype(F32)
                + second_in[k, 1, :, span].astype(F32)
            )

        gate, up, back = total(0), total(1), total(2)
        sig = jax.nn.sigmoid(gate)
        silu = gate * sig
        acts[k, x, :, :FF] = (silu * up).astype(BF16)
        acts[k, x, :, FF : 2 * FF] = (
            back * up * sig * (1.0 + gate * (1.0 - sig))
        ).astype(BF16)
        acts[k, x, :, 2 * FF :] = (back * silu).astype(BF16)
        for i in range(2):
            hop(2, k, i, acts.at[k, x], acts.at[k, x])

    def stage_forward(k):
        for i in range(2):
            ring[2, k, i].wait_recv()
        for i in range(2):
            piece = acts.at[k, near[1 - i], :, halves(i)]
            hop(3, k, i, piece, piece)

    def stage_home(k):
        for i in range(2):
            ring[3, k, i].wait_recv()
        h = acts[k].reshape(ROWS, WIDE)
        out = dot(h[:, :FF], down_ref[...]).astype(BF16)
        back = (
            dot(h[:, FF : 2 * FF], gate_ref[...]) + dot(h[:, 2 * FF :], up_ref[...])
        ).astype(BF16)
        for a in range(SOURCES // 16):
            span = slice(32 * a, 32 * (a + 1))
            stack = jnp.concatenate(
                [out[span, g * 128 : (g + 1) * 128] for g in range(4)]
                + [back[span, g * 128 : (g + 1) * 128] for g in range(4)],
                axis=0,
            )
            home_box[k, 16 * a : 16 * (a + 1)] = (
                dot(spread[...], stack).astype(BF16).reshape(16, 16, 128)
            )
        for j in range(8 // CHUNKS):
            q = k * (8 // CHUNKS) + j

            for i in range(1 if q == 0 else 0, 16):
                push(
                    home_box.at[k, j * 16 + turned[i]],
                    back_box.at[k, j * 16 + yc],
                    home_send,
                    home_recv.at[k],
                    plane(8 - ORDER[q], turned[i]),
                )
        if k == 0:
            copy = pltpu.make_async_copy(
                home_box.at[0, yc], back_box.at[0, yc], local_sem.at[1]
            )
            copy.start()
            ring["home"] = copy

    stages = (stage_partial, stage_sum, stage_act, stage_forward, stage_home)
    for t in range(CHUNKS + len(stages) - 1):
        for s in range(len(stages)):
            if 0 <= t - s < CHUNKS:
                stages[s](t - s)
        if 1 <= t <= 4:
            weigh(2 * t - 2)
            weigh(2 * t - 1)

    h_all = acts[...].reshape(256, WIDE)
    x_all = xin[...].reshape(256, 2 * COLUMNS)

    def outer(a, b):
        return lax.dot_general(
            a, b, (((0,), (0,)), ((), ())), preferred_element_type=F32
        ).astype(BF16)

    grad_gate_ref[...] = outer(h_all[:, FF : 2 * FF], x_all[:, :COLUMNS])
    grad_up_ref[...] = outer(h_all[:, 2 * FF :], x_all[:, :COLUMNS])
    grad_down_ref[...] = outer(h_all[:, :FF], x_all[:, COLUMNS:])

    total = jnp.zeros((128, 128), F32)
    for k in range(CHUNKS):
        if k == 0:
            ring["home"].wait()
            wait_bytes(back_box.at[0, pl.ds(0, SOURCES - 1)], home_recv.at[0])
        else:
            wait_bytes(back_box.at[k], home_recv.at[k])
        block = back_box[k].reshape(SOURCES * 16, 128)
        span = slice(k * SOURCES * 16, (k + 1) * SOURCES * 16)
        total = total + dot(back_hi[:, span], block) + dot(back_lo[:, span], block)
    result = total.astype(BF16)
    for g in range(4):
        mixed_ref[:, g * 128 : (g + 1) * 128] = result[16 * g : 16 * (g + 1)]
        grad_ref[:, g * 128 : (g + 1) * 128] = result[64 + 16 * g : 64 + 16 * (g + 1)]

    for stage in range(5):
        for k in range(CHUNKS):
            for i in range(2):
                ring[stage, k, i].wait_send()
    wait_bytes(out_box.at[pl.ds(0, 7)], send_sem)
    wait_bytes(out_box.at[0, pl.ds(0, 15)], send_sem)
    wait_bytes(back_box.at[pl.ds(0, CHUNKS - 1)], home_send)
    wait_bytes(back_box.at[0, pl.ds(0, SOURCES - 1)], home_send)


def store(*refs):
    sources, targets, sems = refs[:5], refs[5:10], refs[10]
    copies = [
        pltpu.make_async_copy(src, dst, sems.at[i])
        for i, (src, dst) in enumerate(zip(sources, targets))
    ]
    for copy in copies:
        copy.start()
    for copy in copies:
        copy.wait()


def on_device(tokens, cotangent, expert_ids, gate_probs, w_gate, w_up, w_down):
    vmem = pl.BlockSpec(memory_space=pltpu.VMEM)
    hbm = pl.BlockSpec(memory_space=pl.ANY)
    far = pl.BlockSpec(memory_space=pltpu.MemorySpace.HBM)

    def buf(*shape):
        return pltpu.VMEM(shape, BF16)

    dma = pltpu.SemaphoreType.DMA
    results = pl.pallas_call(
        routed,
        out_shape=(
            jax.ShapeDtypeStruct((16, COLUMNS), BF16),
            jax.ShapeDtypeStruct((16, COLUMNS), BF16),
            jax.ShapeDtypeStruct((FF, COLUMNS), BF16),
            jax.ShapeDtypeStruct((FF, COLUMNS), BF16),
            jax.ShapeDtypeStruct((FF, COLUMNS), BF16),
        ),
        in_specs=[far] * 7,
        out_specs=(vmem,) * 5,
        scratch_shapes=[
            pltpu.VMEM((8, 16), jnp.int32),
            pltpu.VMEM((8, 16), F32),
            buf(16, COLUMNS),
            buf(16, COLUMNS),
            buf(CHUNKS, ROWS, 2 * COLUMNS),
            buf(CHUNKS, 4, PIECE, WIDE),
            buf(FF, COLUMNS),
            buf(FF, COLUMNS),
            buf(FF, COLUMNS),
            buf(8, 16, 16, 128),
            buf(CHUNKS, SOURCES, 16, 128),
            buf(CHUNKS, SOURCES, 16, 128),
            buf(CHUNKS, SOURCES, 16, 128),
            buf(128, 2048),
            buf(128, 2048),
            buf(256, 256),
            buf(256, 256),
            buf(CHUNKS, 4, PIECE, WIDE),
            buf(CHUNKS, PIECE, WIDE),
            buf(CHUNKS, 2, PIECE, HALF),
            buf(CHUNKS, 2, PIECE, WIDE),
            dma((7,)),
            dma((2,)),
            dma,
            dma((CHUNKS,)),
            dma,
            dma((CHUNKS,)),
            dma((5, CHUNKS, 2)),
            dma((5, CHUNKS, 2)),
            pltpu.SemaphoreType.REGULAR((8,)),
        ],
        compiler_params=pltpu.CompilerParams(
            collective_id=0, has_side_effects=True, vmem_limit_bytes=51 * 1024 * 1024
        ),
    )(*[pltpu.with_memory_space_constraint(a, pltpu.MemorySpace.HBM) for a in (expert_ids.T, gate_probs.T, tokens, cotangent, w_gate, w_up, w_down)])
    shapes = [jax.ShapeDtypeStruct(r.shape, r.dtype) for r in results]
    mixed, grad_tokens, grad_gate, grad_up, grad_down = pl.pallas_call(
        store,
        out_shape=shapes,
        in_specs=[vmem] * 5,
        out_specs=[hbm] * 5,
        scratch_shapes=[dma((5,))],
        compiler_params=pltpu.CompilerParams(vmem_limit_bytes=4 * 1024 * 1024),
    )(*results)
    return (mixed, grad_tokens, grad_gate[None], grad_up[None], grad_down[None])


def solution(mesh):
    in_specs = (
        P("expert", "dp"),
        P("expert", "dp"),
        P("expert", None),
        P("expert", None),
        P("expert", None, "dp"),
        P("expert", None, "dp"),
        P("expert", None, "dp"),
    )
    out_specs = (
        P("expert", "dp"),
        P("expert", "dp"),
        P("expert", None, "dp"),
        P("expert", None, "dp"),
        P("expert", None, "dp"),
    )
    return jax.shard_map(
        on_device, mesh=mesh, in_specs=in_specs, out_specs=out_specs, check_vma=False
    )
```
